128 devices in a mesh: region: 4 (over x), sub: 32 (over y, z, core).
Axes of the slice: x: 4, y: 4, z: 4, core: 2. Of those that a mesh axis runs over, the one named last changes fastest.
Arguments:
- scalars: float32 [16384, 128], P(('region', 'sub')), may hold values from -6 to 6
- vectors: float32 [3, 16384, 128], P(None, ('region', 'sub')), may hold values from -6 to 6
- positions: float32 [3, 16384], P(None, ('region', 'sub')), may hold values from 0 to 8
- pair_blocks: int32 [2, 192], replicated, may hold values from 0 to 127, as said below
- pair_mask: int32 [192, 547], replicated, may hold values from 0 to 1073741823
- wavevectors: float32 [3, 512], replicated, may hold values from -2 to 2
- message_in: float32 [2, 128, 128], replicated, may hold values from -0.5 to 0.5
- message_out: float32 [2, 128, 384], replicated, may hold values from -0.5 to 0.5
- filter_weight: float32 [2, 20, 384], replicated, may hold values from -0.3125 to 0.3125
- ewald_weight: float32 [2, 128, 128], replicated, may hold values from -0.5 to 0.5
- ewald_filter: float32 [2, 512, 128], replicated, may hold values from -6 to 6
- mixing_left: float32 [2, 128, 128], replicated, may hold values from -0.5 to 0.5
- mixing_right: float32 [2, 128, 128], replicated, may hold values from -0.5 to 0.5
- update_in: float32 [2, 256, 128], replicated, may hold values from -0.375 to 0.375
- update_out: float32 [2, 128, 384], replicated, may hold values from -0.5 to 0.5
Outputs:
- scalars_out: float32 [16384, 128], P(('region', 'sub'))
- vectors_out: float32 [3, 16384, 128], P(None, ('region', 'sub'))
The draws below stay inside these ranges and needn't reach their ends.
Inputs may be any that keep to these rules, and one draw needn't show every extreme that they name: `pair_blocks`: pairs are listed region by region, 48 pairs for each of the 4 regions of 32 consecutive blocks. Both blocks of a pair lie in the same region, the first below the second; no pair is listed twice, and within a region the first blocks never fall along the list.
All inputs are finite; a program needn't handle non-finite values.
Results may differ from the reference program's by a relative error of at most 0.0003.
Values sent between devices are 32-bit elements; how exact they have to be, the bound alone decides.
A program may use at most 128 MiB of HBM per device.

```python
import math
import jax
import jax.numpy as jnp
import numpy as np
from jax import lax

F = 128
NRBF = 20
BS = 128
KW = 512
LAYERS = 2
REGIONS = 4
REGION_BLOCKS = 32
NATOM = 16384
RPAIRS = 48
PAIRS = 192
MASKW = 547


def pair_table(key):
    upper_first, upper_second = np.triu_indices(REGION_BLOCKS, 1)
    first_table = jnp.asarray(upper_first.astype(np.int32))
    second_table = jnp.asarray(upper_second.astype(np.int32))
    combos = upper_first.shape[0]
    corner = REGION_BLOCKS - 2
    firsts = []
    seconds = []
    for region in range(REGIONS):
        others = jax.random.permutation(jax.random.fold_in(key, 11 + region), combos - 1)[:RPAIRS - 1]
        others = others + (others >= corner).astype(others.dtype)
        chosen = jnp.concatenate([others, jnp.full((1,), corner, others.dtype)])
        chosen = jnp.sort(chosen)
        firsts.append(first_table[chosen] + region * REGION_BLOCKS)
        seconds.append(second_table[chosen] + region * REGION_BLOCKS)
    return jnp.stack([jnp.concatenate(firsts), jnp.concatenate(seconds)]).astype(jnp.int32)


def draw_pair_blocks(key, part):
    return pair_table(key)


def place_ends(values, rng, smallest, top_value):
    extent = values.shape
    index_at = [jax.random.randint(jax.random.fold_in(rng, axis), (), 0, extent[axis]) for axis in range(len(extent))]
    values = values.at[tuple(index_at)].set(smallest)
    longest = extent.index(max(extent))
    index_at[longest] = (index_at[longest] + 1) % extent[longest]
    return values.at[tuple(index_at)].set(top_value)


def steps_of(stream_key, shape, shards, low, largest):
    def one(axis_at, shards_of):
        heights = jax.random.uniform(jax.random.fold_in(jax.random.fold_in(stream_key, 6), axis_at), (shards_of,), jnp.float32, low / len(shards), largest / len(shards))
        return jnp.repeat(jnp.exp(heights), shape[axis_at] // shards_of).reshape((-1,) + (1,) * (len(shape) - axis_at - 1))

    gain = one(*shards[0])
    for cut in shards[1:]:
        gain = gain * one(*cut)
    return gain


def gaussian(stream_key, shape, width, limit, shards=(), kind=jnp.bfloat16):
    result = jax.random.normal(stream_key, shape, jnp.float32) * width
    if len(shards) > 0:
        result = steps_of(stream_key, shape, shards, -0.22, 0.18) * result
    return jnp.clip(result, min=-limit, max=limit).astype(kind)


def setup_inputs(seed: int = 0) -> dict:
    streams_of = jax.random.split(jax.random.key(seed), 16)
    scalars = gaussian(streams_of[0], (NATOM, F), 1.0, 6.0, ((0, 128),), jnp.float32)
    vectors = gaussian(streams_of[1], (3, NATOM, F), 1.0, 6.0, ((1, 128),), jnp.float32)
    positions = jnp.clip(8.0 * jax.random.uniform(streams_of[2], (3, NATOM), jnp.float32) ** steps_of(streams_of[2], (3, NATOM), ((1, 128),), -0.2, 0.2), 0.0, 8.0)
    pair_blocks = draw_pair_blocks(jax.random.fold_in(streams_of[15], 71), 0)
    pair_mask = place_ends(jax.random.randint(streams_of[4], (PAIRS, MASKW), 0, 1073741824), jax.random.fold_in(streams_of[4], 1), 0, 1073741823).astype(jnp.int32)
    wavevectors = jnp.clip(jax.random.uniform(streams_of[5], (3, KW), jnp.float32, -2.0, 2.0), -2.0, 2.0)
    message_in = gaussian(streams_of[6], (LAYERS, F, F), F ** -0.5, 0.5, (), jnp.float32)
    message_out = gaussian(streams_of[7], (LAYERS, F, 3 * F), F ** -0.5, 0.5, (), jnp.float32)
    filter_weight = gaussian(streams_of[8], (LAYERS, NRBF, 3 * F), (16 * NRBF) ** -0.5, 0.3125, (), jnp.float32)
    ewald_weight = gaussian(streams_of[9], (LAYERS, F, F), F ** -0.5, 0.5, (), jnp.float32)
    ewald_filter = gaussian(streams_of[10], (LAYERS, KW, F), 1.0, 6.0, (), jnp.float32)
    mixing_left = gaussian(streams_of[11], (LAYERS, F, F), F ** -0.5, 0.5, (), jnp.float32)
    mixing_right = gaussian(streams_of[12], (LAYERS, F, F), F ** -0.5, 0.5, (), jnp.float32)
    update_in = gaussian(streams_of[13], (LAYERS, 2 * F, F), (2 * F) ** -0.5, 0.375, (), jnp.float32)
    update_out = gaussian(streams_of[14], (LAYERS, F, 3 * F), F ** -0.5, 0.5, (), jnp.float32)
    return {"scalars": scalars, "vectors": vectors, "positions": positions, "pair_blocks": pair_blocks, "pair_mask": pair_mask, "wavevectors": wavevectors, "message_in": message_in, "message_out": message_out, "filter_weight": filter_weight, "ewald_weight": ewald_weight, "ewald_filter": ewald_filter, "mixing_left": mixing_left, "mixing_right": mixing_right, "update_in": update_in, "update_out": update_out}


HIGHEST = lax.Precision.HIGHEST
CUTOFF = 8.0

def unpack_mask(packed):
    shifts = jnp.arange(30, dtype=jnp.int32)
    unpacked = jnp.right_shift(packed[:, None], shifts[None, :]) & 1
    return unpacked.reshape(-1)[:BS * BS].reshape(BS, BS).astype(jnp.float32)

def geometry(pos_first, pos_second, packed):
    offset = pos_second[:, None, :] - pos_first[:, :, None]
    distance = jnp.sqrt(lax.optimization_barrier(jnp.sum(offset * offset, axis=0)) + 1.0)
    direction = offset / distance[None]
    spacing = CUTOFF / (NRBF - 1)
    centers = jnp.arange(NRBF, dtype=jnp.float32) * spacing
    scaled = (distance[None] - centers[:, None, None]) / spacing
    radial = jnp.exp(-0.5 * scaled * scaled) * unpack_mask(packed)[None]
    return (radial, direction)

def side_terms(radial, direction, source, filters):
    channels = source.shape[1] // 5
    rows = radial.shape[1]
    product = jnp.dot(radial.reshape(-1, radial.shape[2]), source, precision=HIGHEST)
    product = product.reshape(NRBF, rows, 5 * channels)
    steered = (direction[:, None] * radial[None]).reshape(-1, radial.shape[2])
    turned = jnp.dot(steered, source[:, 4 * channels:], precision=HIGHEST).reshape(3, NRBF, rows, channels)
    w_scalar = filters[:, :channels]
    w_vector = filters[:, channels:2 * channels]
    w_radial = filters[:, 2 * channels:]
    delta_scalar = jnp.einsum('kic,kc->ic', product[..., :channels], w_scalar, precision=HIGHEST)
    parts = []
    for component in range(3):
        lower = (1 + component) * channels
        along = jnp.einsum('kic,kc->ic', product[..., lower:lower + channels], w_vector, precision=HIGHEST)
        along = along + jnp.einsum('kic,kc->ic', turned[component], w_radial, precision=HIGHEST)
        parts.append(along)
    return (delta_scalar, jnp.stack(parts))

def pair_terms(radial, direction, source_first, source_second, filters):
    to_first = side_terms(radial, direction, source_second, filters)
    to_second = side_terms(radial.transpose(0, 2, 1), -direction.transpose(0, 2, 1), source_first, filters)
    return (to_first, to_second)

def message_sources(scalars_now, vectors_now, first_weight, second_weight):
    channels = scalars_now.shape[1]
    hidden = jax.nn.silu(jnp.dot(scalars_now, first_weight, precision=HIGHEST))
    filt_in = jnp.dot(hidden, second_weight, precision=HIGHEST)
    phi_vector = filt_in[:, channels:2 * channels]
    return jnp.concatenate([filt_in[:, :channels], phi_vector * vectors_now[0], phi_vector * vectors_now[1], phi_vector * vectors_now[2], filt_in[:, 2 * channels:]], axis=1)

def update_block(mid_scalars, mid_vectors, left_weight, right_weight, gate_in, gate_out):
    channels = mid_scalars.shape[1]
    flat = mid_vectors.reshape(-1, channels)
    left = jnp.dot(flat, left_weight, precision=HIGHEST).reshape(mid_vectors.shape)
    right = jnp.dot(flat, right_weight, precision=HIGHEST).reshape(mid_vectors.shape)
    vec_norm = jnp.sqrt(lax.optimization_barrier(jnp.sum(right * right, axis=0)) + 1.0)
    hidden = jax.nn.silu(jnp.dot(jnp.concatenate([mid_scalars, vec_norm], axis=1), gate_in, precision=HIGHEST))
    gates = jnp.dot(hidden, gate_out, precision=HIGHEST)
    new_vectors = mid_vectors + gates[None, :, :channels] * left
    new_scalars = mid_scalars + gates[:, channels:2 * channels] * lax.optimization_barrier(jnp.sum(left * right, axis=0)) + gates[:, 2 * channels:]
    return (new_scalars, new_vectors)

def add_rows(target, delta, row_at, axis_id):
    current = lax.dynamic_slice_in_dim(target, row_at, BS, axis_id)
    return lax.dynamic_update_slice_in_dim(target, current + delta, row_at, axis_id)

def reference(scalars, vectors, positions, pair_blocks, pair_mask, wavevectors, message_in, message_out, filter_weight, ewald_weight, ewald_filter, mixing_left, mixing_right, update_in, update_out):
    natoms = scalars.shape[0]
    phases = jnp.dot(wavevectors.T, positions, precision=HIGHEST)
    cosines = jnp.cos(phases)
    sines = jnp.sin(phases)
    scale = 1.0 / math.sqrt(natoms * KW)
    scalars_now, vectors_now = (scalars, vectors)
    for layer_id in range(LAYERS):
        sources = message_sources(scalars_now, vectors_now, message_in[layer_id], message_out[layer_id])
        filters = filter_weight[layer_id]

        def visit(pair_id, totals):
            sum_scalar, sum_vector = totals
            first_row = (pair_blocks[0, pair_id] * BS).astype(jnp.int32)
            second_row = (pair_blocks[1, pair_id] * BS).astype(jnp.int32)
            pos_first = lax.dynamic_slice_in_dim(positions, first_row, BS, 1)
            pos_second = lax.dynamic_slice_in_dim(positions, second_row, BS, 1)
            radial, direction = geometry(pos_first, pos_second, pair_mask[pair_id])
            source_first = lax.dynamic_slice_in_dim(sources, first_row, BS, 0)
            source_second = lax.dynamic_slice_in_dim(sources, second_row, BS, 0)
            to_first, to_second = pair_terms(radial, direction, source_first, source_second, filters)
            sum_scalar = add_rows(sum_scalar, to_first[0], first_row, 0)
            sum_scalar = add_rows(sum_scalar, to_second[0], second_row, 0)
            sum_vector = add_rows(sum_vector, to_first[1], first_row, 1)
            sum_vector = add_rows(sum_vector, to_second[1], second_row, 1)
            return (sum_scalar, sum_vector)
        start = (jnp.zeros(scalars_now.shape, jnp.float32), jnp.zeros(vectors_now.shape, jnp.float32))
        delta_scalar, delta_vector = lax.fori_loop(0, pair_blocks.shape[1], visit, start)
        charges = jnp.dot(scalars_now, ewald_weight[layer_id], precision=HIGHEST)
        structure_re = jnp.dot(cosines, charges, precision=HIGHEST)
        structure_im = jnp.dot(sines, charges, precision=HIGHEST)
        ewald = jnp.dot(cosines.T, ewald_filter[layer_id] * structure_re, precision=HIGHEST)
        ewald = (ewald + jnp.dot(sines.T, ewald_filter[layer_id] * structure_im, precision=HIGHEST)) * scale
        mid_scalars = scalars_now + delta_scalar + ewald
        mid_vectors = vectors_now + delta_vector
        scalars_now, vectors_now = update_block(mid_scalars, mid_vectors, mixing_left[layer_id], mixing_right[layer_id], update_in[layer_id], update_out[layer_id])
    return (scalars_now, vectors_now)
```

```python
import functools
import math

import jax
import jax.numpy as jnp
from jax import lax
from jax.experimental import pallas as pl
from jax.experimental.pallas import tpu as pltpu
from jax.sharding import PartitionSpec as P

NRBF = 20
BS = 128
KW = 512
LAYERS = 2
CUTOFF = 8.0
SPACING = CUTOFF / (NRBF - 1)
CENTRE = 4.0
ROWS15 = 15
RATE = math.sqrt(0.5 * math.log2(math.e))
KCHUNK = 5
SCALE = 1.0 / math.sqrt(16384 * KW)

BF16 = jnp.bfloat16
F32 = jnp.float32


def far(x):
    return pltpu.with_memory_space_constraint(x, pltpu.HBM)


def split2(x):
    high = x.astype(BF16)
    low = (x - high.astype(F32)).astype(BF16)
    return high, low


def left3(x):
    high, low = split2(x)
    return jnp.concatenate([high, low, high], axis=1)


def right3(x):
    high, low = split2(x)
    return jnp.concatenate([high, high, low], axis=0)


def dot3(x, weights):
    return jnp.dot(left3(x), weights, preferred_element_type=F32)


EXCHANGE_VMEM = 24 << 20
PAIR_VMEM = 36 << 20
MESH = pl.DeviceIdType.MESH
HALF = BS // 2
SROWS = BS + 8


def waves_of(phase):
    count = jnp.floor(phase * (2.0 / math.pi) + 0.5)
    rest = phase - count * 1.5703125
    rest = rest - count * 4.837512969970703125e-4
    rest = rest - count * 7.549789948768648e-8
    square = rest * rest
    sine = rest + rest * square * (
        -1.6666654611e-1 + square * (8.3321608736e-3 - square * 1.9515295891e-4)
    )
    cosine = (
        1.0
        - 0.5 * square
        + square
        * square
        * (4.166664568298827e-2 + square * (-1.388731625493765e-3 + square * 2.443315711809948e-5))
    )

    def pick(ahead):
        quarter = count + ahead
        half = jnp.floor(quarter * 0.5)
        odd = quarter - 2.0 * half
        sign = 1.0 - 2.0 * (half - 2.0 * jnp.floor(half * 0.5))
        return sign * (sine + odd * (cosine - sine))

    return pick(1.0), pick(0.0)


def exchange_kernel(first_layer, layer, *refs):
    if first_layer:
        (s_hbm, pos_hbm, v_hbm, wide_hbm, ew_hbm) = refs[:5]
        (sp_all, v_all, s_all, trig, own_trig) = refs[5:10]
        rest = refs[10:]
        (wide_ref, wave_ref) = rest[-2:]
        rest = rest[:-2]
    else:
        (sp_ref, v_ref, trig, ew_hbm) = refs[:4]
        (sp_all, v_all, s_all) = refs[4:7]
        rest = refs[7:]
    (cross, ew_ref, send_sem, recv_sem, own_sem, x_send, x_recv, p_send, p_recv) = rest
    region = lax.axis_index("region")
    sub = lax.axis_index("sub")
    keep = [pltpu.make_async_copy(ew_hbm.at[layer], ew_ref, own_sem.at[0])]
    if first_layer:
        fetch = [
            pltpu.make_async_copy(s_hbm, sp_all.at[sub, pl.ds(0, BS), :], own_sem.at[1]),
            pltpu.make_async_copy(pos_hbm, sp_all.at[sub, pl.ds(BS, 3), :], own_sem.at[2]),
            pltpu.make_async_copy(v_hbm, v_all.at[sub], own_sem.at[3]),
            pltpu.make_async_copy(wide_hbm, wide_ref, own_sem.at[4]),
        ]
    else:
        fetch = []
        keep.append(pltpu.make_async_copy(sp_ref, sp_all.at[sub], own_sem.at[1]))
        keep.append(pltpu.make_async_copy(v_ref, v_all.at[sub], own_sem.at[2]))
    for copy in keep + fetch:
        copy.start()
    core = lax.rem(sub, 2)
    z = lax.rem(sub // 2, 4)
    y = sub // 8
    fwd = 1 + 2 * core
    bwd = 3 - 2 * core

    def device(dy, dz, other=False):
        use = 1 - core if other else core
        return (lax.rem(y + dy, 4) * 4 + lax.rem(z + dz, 4)) * 2 + use

    def place(half, one, two):
        return device(two, one) if half == 0 else device(one, two)

    partner = device(0, 0, True)
    barrier = pltpu.get_barrier_semaphore()
    peers = [(region, partner)]
    for step in range(1, 4):
        peers.append((region, device(step, 0)))
        peers.append((region, device(0, step)))
        peers.append((lax.rem(region + step, 4), sub))
    for peer in peers:
        pl.semaphore_signal(barrier, inc=1, device_id=peer, device_id_type=MESH)
    pl.semaphore_wait(barrier, len(peers))

    def piece(kind, half, dev):
        if kind == 0:
            if half == 0:
                return sp_all.at[dev, pl.ds(0, HALF), :]
            return sp_all.at[dev, pl.ds(HALF, SROWS - HALF), :]
        return v_all.at[dev, :, pl.ds(half * HALF, HALF), :]

    def own_piece(kind, half):
        if kind == 0:
            if half == 0:
                return sp_ref.at[pl.ds(0, HALF), :]
            return sp_ref.at[pl.ds(HALF, SROWS - HALF), :]
        return v_ref.at[:, pl.ds(half * HALF, HALF), :]

    sent = []

    def send(kind, half, dev, target, own=False):
        copy = pltpu.make_async_remote_copy(
            src_ref=own_piece(kind, half) if own and not first_layer else piece(kind, half, dev),
            dst_ref=piece(kind, half, dev),
            send_sem=send_sem.at[len(sent)],
            recv_sem=recv_sem.at[kind * 2 + half, dev],
            device_id=(region, target),
            device_id_type=MESH,
        )
        copy.start()
        sent.append(copy)

    def arrive(kind, half, dev):
        pltpu.make_async_remote_copy(
            src_ref=piece(kind, half, dev),
            dst_ref=piece(kind, half, dev),
            send_sem=send_sem.at[0],
            recv_sem=recv_sem.at[kind * 2 + half, dev],
            device_id=(region, partner),
            device_id_type=MESH,
        ).wait_recv()

    def own_sends(kind, stage):
        for half in range(2):
            for way in (fwd, bwd):
                target = place(half, way, 0) if stage == 0 else place(half, 0, way)
                send(kind, half, sub, target, own=True)

    def own_partner(kind):
        for half in range(2):
            send(kind, half, sub, partner, own=True)

    def second(kind, half, dev):
        send(kind, half, dev, place(half, 0, fwd))
        send(kind, half, dev, place(half, 0, bwd))
        send(kind, half, dev, partner)

    def near_first(kind, ways_now):
        for half in range(2):
            for way in ways_now:
                dev = place(half, way, 0)
                arrive(kind, half, dev)
                if kind == 0 and way is bwd:
                    send(kind, half, dev, place(half, fwd, 0))
                if kind == 1 and way is fwd:
                    send(kind, half, dev, place(half, bwd, 0))
                second(kind, half, dev)

    def far_first(kind):
        for half in range(2):
            dev = place(half, 2, 0)
            arrive(kind, half, dev)
            second(kind, half, dev)

    def near_second(kind, one):
        for half in range(2):
            dev = place(half, one, bwd)
            arrive(kind, half, dev)
            if kind == 0:
                send(kind, half, dev, place(half, 0, fwd))
            send(kind, half, dev, partner)
            dev = place(half, one, fwd)
            arrive(kind, half, dev)
            if kind == 1:
                send(kind, half, dev, place(half, 0, bwd))
            send(kind, half, dev, partner)

    def far_second(kind, one):
        for half in range(2):
            dev = place(half, one, 2)
            arrive(kind, half, dev)
            send(kind, half, dev, partner)

    def from_partner(kind):
        for half in range(2):
            for dy in range(4):
                for dz in range(4):
                    arrive(kind, half, device(dy, dz, True))

    slot = core * 16 + y * 4 + z
    for copy in fetch[:2]:
        copy.wait()
    own_sends(0, 0)
    own_sends(0, 1)
    own_partner(0)
    for copy in fetch[2:]:
        copy.wait()
    own_sends(1, 0)
    if first_layer:
        column = sp_all[sub, BS : BS + 8, :].T
        phase = (
            column[:, 0:1] * wide_ref[0:1, :]
            + column[:, 1:2] * wide_ref[1:2, :]
            + column[:, 2:3] * wide_ref[2:3, :]
        )
        cosines, sines = waves_of(phase)
        own_trig[:, 0:KW] = cosines
        own_trig[:, KW:] = sines
        wave_ref[...] = jnp.concatenate([wide_ref[...], jnp.zeros((5, KW), F32)], axis=0).T
    ways = (0, bwd, fwd, 2)
    near_first(0, (bwd, fwd))
    own_sends(1, 1)
    far_first(0)
    for one in ways[:3]:
        near_second(0, one)
    near_first(1, (fwd,))
    near_second(0, 2)
    near_first(1, (bwd,))
    own_partner(1)
    for one in ways:
        far_second(0, one)
    near_second(1, 0)
    for copy in keep:
        copy.wait()
    from_partner(0)
    far_first(1)
    if first_layer:
        wave = wave_ref[pl.ds(pl.multiple_of(slot * 16, 16), 16), :]

    def gather_structure(step, total):
        if first_layer:
            sides = []
            for n in range(2):
                pos = sp_all[2 * step + n, BS : BS + 8, :]
                phase = (
                    wave[:, 0:1] * pos[0:1, :]
                    + wave[:, 1:2] * pos[1:2, :]
                    + wave[:, 2:3] * pos[2:3, :]
                )
                sides.append(jnp.concatenate(waves_of(phase), axis=0))
            waves = jnp.concatenate(sides, axis=1)
            trig[step] = waves
        else:
            waves = trig[step]
        atoms = jnp.concatenate(
            [sp_all[2 * step, 0:BS, :], sp_all[2 * step + 1, 0:BS, :]], axis=0
        )
        wave_high, wave_low = split2(waves)
        atom_high, atom_low = split2(atoms)
        both = jnp.dot(
            jnp.concatenate([wave_high, wave_low], axis=0),
            atom_high,
            preferred_element_type=F32,
        )
        low = jnp.dot(wave_high, atom_low, preferred_element_type=F32)
        return total + (both[:32] + both[32:] + low)

    structure = lax.fori_loop(0, 16, gather_structure, jnp.zeros((32, BS), F32), unroll=4)
    cross[0] = dot3(structure, right3(ew_ref[...]))
    across = []
    for step in range(1, 4):
        copy = pltpu.make_async_remote_copy(
            src_ref=cross.at[0],
            dst_ref=cross.at[4 - step],
            send_sem=x_send.at[step - 1],
            recv_sem=x_recv.at[4 - step - 1],
            device_id=(lax.rem(region + step, 4), sub),
            device_id_type=MESH,
        )
        copy.start()
        across.append(copy)
    for one in ways[1:3]:
        near_second(1, one)
    for copy in across:
        copy.wait()
    s_all[slot] = cross[0] + cross[1] + cross[2] + cross[3]
    line = []
    for step in range(1, 4):
        copy = pltpu.make_async_remote_copy(
            src_ref=s_all.at[slot],
            dst_ref=s_all.at[slot],
            send_sem=p_send.at[step - 1],
            recv_sem=p_recv.at[step - 1],
            device_id=(region, device(0, step)),
            device_id_type=MESH,
        )
        copy.start()
        line.append(copy)
    near_second(1, 2)
    for copy in line:
        copy.wait()
    plane = []
    mine = s_all.at[pl.ds(core * 16 + y * 4, 4)]
    for step in range(1, 4):
        copy = pltpu.make_async_remote_copy(
            src_ref=mine,
            dst_ref=mine,
            send_sem=p_send.at[2 + step],
            recv_sem=p_recv.at[2 + step],
            device_id=(region, device(step, 0)),
            device_id_type=MESH,
        )
        copy.start()
        plane.append(copy)
    for one in ways:
        far_second(1, one)
    for copy in plane:
        copy.wait()
    side = s_all.at[pl.ds(core * 16, 16)]
    last = pltpu.make_async_remote_copy(
        src_ref=side,
        dst_ref=side,
        send_sem=p_send.at[6],
        recv_sem=p_recv.at[6],
        device_id=(region, partner),
        device_id_type=MESH,
    )
    last.start()
    from_partner(1)
    last.wait()
    for copy in sent:
        copy.wait_send()


SENDS = 124


def exchange(first_layer, layer, *args):
    vmem = pl.BlockSpec(memory_space=pltpu.VMEM)
    hbm = pl.BlockSpec(memory_space=pltpu.HBM)
    shapes = [(32, SROWS, BS), (32, 3, BS, BS), (32, 32, BS)]
    if first_layer:
        shapes += [(16, 32, 2 * BS), (BS, 2 * KW)]
    return pl.pallas_call(
        functools.partial(exchange_kernel, first_layer, layer),
        out_shape=tuple(jax.ShapeDtypeStruct(shape, F32) for shape in shapes),
        in_specs=[hbm] * 5 if first_layer else [vmem] * 3 + [hbm],
        out_specs=(vmem,) * len(shapes),
        scratch_shapes=[
            pltpu.VMEM((4, 32, BS), F32),
            pltpu.VMEM((BS, BS), F32),
            pltpu.SemaphoreType.DMA((SENDS,)),
            pltpu.SemaphoreType.DMA((4, 32)),
            pltpu.SemaphoreType.DMA((5,)),
            pltpu.SemaphoreType.DMA((3,)),
            pltpu.SemaphoreType.DMA((3,)),
            pltpu.SemaphoreType.DMA((7,)),
            pltpu.SemaphoreType.DMA((7,)),
        ]
        + ([pltpu.VMEM((3, KW), F32), pltpu.VMEM((KW, 8), F32)] if first_layer else []),
        compiler_params=pltpu.CompilerParams(
            collective_id=layer, has_side_effects=True, vmem_limit_bytes=EXCHANGE_VMEM
        ),
        name="exchange_first" if first_layer else "exchange_next",
    )(*args)


def pair_kernel(layer, n_region, *refs):
    (
        pb_hbm,
        mask_hbm,
        sp_ref,
        v_ref,
        st_ref,
        trig_ref,
        w1_hbm,
        w2_hbm,
        filt_hbm,
        ef_hbm,
        ml_hbm,
        mr_hbm,
        ui_hbm,
        uo_hbm,
        out_s_ref,
        out_v_ref,
        pb_ref,
        mask_ref,
        w1_ref,
        w2_ref,
        filt_ref,
        ef_ref,
        ml_ref,
        mr_ref,
        ui_ref,
        uo_ref,
        sem,
        ds_ref,
        dv_ref,
        structure,
        onehot,
        w1c,
        w2c,
        filt_a,
        filt_b,
        mask_pad,
        src_a,
        src_b,
        left_a,
        left_b,
        acc_a,
        acc_b,
        todo,
    ) = refs
    pairs = pb_hbm.shape[1] // n_region
    region = lax.axis_index("region")
    base = lax.axis_index("sub")
    list_move = pltpu.make_async_copy(pb_hbm, pb_ref, sem.at[8])
    list_move.start()
    mask_move = pltpu.make_async_copy(mask_hbm.at[pl.ds(region * pairs, pairs)], mask_ref, sem.at[9])
    mask_move.start()
    moves = []
    for n, (far, near) in enumerate(
        (
            (w1_hbm, w1_ref),
            (w2_hbm, w2_ref),
            (filt_hbm, filt_ref),
            (ef_hbm, ef_ref),
            (ml_hbm, ml_ref),
            (mr_hbm, mr_ref),
            (ui_hbm, ui_ref),
            (uo_hbm, uo_ref),
        )
    ):
        move = pltpu.make_async_copy(far.at[layer], near, sem.at[n])
        move.start()
        moves.append(move)
    blocks = sp_ref.shape[0]
    rows = BS
    flat = lax.broadcasted_iota(jnp.int32, (1, ROWS15 * BS), 1)
    word = (flat * 2185) >> 16
    bit = flat - word * 30
    shift = bit & 7
    onehot[...] = jnp.where(
        lax.broadcasted_iota(jnp.int32, (256, ROWS15 * BS), 0) == (bit >> 3) * 64 + word, 1.0, 0.0
    ).astype(BF16)
    ds_ref[...] = jnp.zeros_like(ds_ref)
    dv_ref[...] = jnp.zeros_like(dv_ref)
    low_lane = lax.broadcasted_iota(jnp.int32, (8, BS), 1) < 64

    list_move.wait()

    def listing(pair, count):
        first = pb_ref[0, region * pairs + pair] - region * blocks
        second = pb_ref[1, region * pairs + pair] - region * blocks

        @pl.when(first == base)
        def _():
            todo[0, count] = second
            todo[1, count] = pair

        @pl.when(second == base)
        def _():
            todo[0, count] = first
            todo[1, count] = pair

        return count + ((first == base) | (second == base)).astype(jnp.int32)

    count = lax.fori_loop(0, pairs, listing, 0)
    todo[0, count] = base
    todo[1, count] = 0
    mask_move.wait()
    for move in moves[:3]:
        move.wait()
    w1c[...] = right3(w1_ref[...])
    w2c[...] = right3(w2_ref[...])
    filt = filt_ref[...]
    filt_a[...] = jnp.concatenate([filt[:, :BS]] + [filt[:, BS : 2 * BS]] * 3, axis=1)
    filt_b[...] = jnp.concatenate([filt[:, 2 * BS :]] * 4, axis=1)
    pos_rcv = sp_ref[base, BS : BS + 8, :]
    col_rcv = pos_rcv.T

    def prepare(term, side):
        source = todo[0, term]
        pair = todo[1, term]
        alive = (term < count).astype(F32)
        line = mask_ref[pl.ds(pair, 1), :]
        short = line.shape[1] - 4 * BS
        last = jnp.concatenate([line[:, 4 * BS :], jnp.zeros((1, BS - short), jnp.int32)], axis=1)
        words = jnp.concatenate(
            [line[:, n * BS : (n + 1) * BS] for n in range(4)] + [last] * 4, axis=0
        )
        bytes4 = [((words >> (8 * q)) & 255).astype(F32) for q in range(4)]
        turned = [pltpu.roll(x, 64, 1) for x in bytes4]
        even = [jnp.where(low_lane, bytes4[q], turned[q + 1]) for q in (0, 2)]
        odd = [jnp.where(low_lane, turned[q], bytes4[q + 1]) for q in (0, 2)]
        packed = jnp.concatenate(
            [jnp.concatenate(even, axis=1), jnp.concatenate(odd, axis=1)], axis=0
        ).astype(BF16)
        found = jnp.dot(packed, onehot[...], preferred_element_type=F32)
        bits = ((found.astype(jnp.int32) >> shift) & 1).astype(F32)
        for r in range(ROWS15):
            for n in range(2):
                mask_pad[side, pl.ds(n * ROWS15 + r, 8, stride=2 * ROWS15), :] = bits[
                    n * 8 : n * 8 + 8, r * BS : (r + 1) * BS
                ]

        straight = (source > base).astype(F32)
        plain = mask_pad[side, 0:BS, :]
        mask = (straight * alive) * plain + ((1.0 - straight) * alive) * plain.T
        hidden = dot3(sp_ref[source, 0:BS, :], w1c[...])
        hidden = hidden / (1.0 + jnp.exp(-hidden))
        phi = dot3(hidden, w2c[...])
        pos_src = sp_ref[source, BS : BS + 8, :]
        col_src = pos_src.T
        phi_v = phi[:, BS : 2 * BS]
        phi_r = phi[:, 2 * BS :]
        parts = [phi[:, :BS]]
        for d in range(3):
            parts.append(phi_v * v_ref[source, d])
        for d in range(3):
            parts.append(phi_r * (col_src[:, d : d + 1] - CENTRE))
        parts.append(phi_r)
        lo = side * BS
        for n, part in enumerate(parts):
            src = src_a if n < 4 else src_b
            high, low = split2(part)
            at = (n % 4) * BS
            src[lo : lo + BS, at : at + BS] = high
            src[2 * BS + lo : 2 * BS + lo + BS, at : at + BS] = low
        square = None
        for d in range(3):
            off = pos_src[d : d + 1, :] - col_rcv[:, d : d + 1]
            square = off * off if square is None else square + off * off
        distance = jnp.sqrt(square + 1.0)
        inverse = 1.0 / distance
        scaled = jnp.where(mask > 0.5, distance * (RATE / SPACING), 1.0e4)
        return scaled, inverse

    def radial(side, chunk, scaled, inverse):
        lo = side * BS
        for k in range(chunk * KCHUNK, (chunk + 1) * KCHUNK):
            away = scaled - RATE * k
            decay = jnp.exp2(-(away * away))
            for left, value in ((left_a, decay), (left_b, decay * inverse)):
                high, low = split2(value)
                left[k * rows : (k + 1) * rows, lo : lo + BS] = high
                left[k * rows : (k + 1) * rows, 2 * BS + lo : 2 * BS + lo + BS] = low

    def visit(step, carry):
        shapes = [prepare(2 * step + side, side) for side in range(2)]
        for chunk in range(NRBF // KCHUNK):
            for side in range(2):
                radial(side, chunk, *shapes[side])
            for acc, left, src, filters in (
                (acc_a, left_a, src_a, filt_a),
                (acc_b, left_b, src_b, filt_b),
            ):
                high = src[0 : 2 * BS, :]
                weights = jnp.concatenate([high, high, src[2 * BS :, :]], axis=0)
                lo = chunk * KCHUNK
                block = left[lo * rows : (lo + KCHUNK) * rows, :]
                product = jnp.dot(
                    jnp.concatenate([block, block[:, : 2 * BS]], axis=1),
                    weights,
                    preferred_element_type=F32,
                )
                total = None
                for k in range(KCHUNK):
                    term = product[k * rows : (k + 1) * rows, :] * filters[lo + k : lo + k + 1, :]
                    total = term if total is None else total + term
                if chunk == 0:
                    acc[...] = total
                else:
                    acc[...] += total
        ds_ref[...] += acc_a[:, :BS]
        tail = acc_b[:, 3 * BS :]
        for d in range(3):
            dv_ref[d] += (
                acc_a[:, (d + 1) * BS : (d + 2) * BS]
                + acc_b[:, d * BS : (d + 1) * BS]
                - (col_rcv[:, d : d + 1] - CENTRE) * tail
            )
        return carry

    lax.fori_loop(0, (count + 1) // 2, visit, 0)
    for move in moves[3:]:
        move.wait()
    for n in range(32):
        for side in range(2):
            lo = side * KW + n * 16
            structure[lo : lo + 16, :] = (
                st_ref[n, side * 16 : side * 16 + 16, :] * ef_ref[n * 16 : n * 16 + 16, :]
            )
    waves_high, waves_low = split2(trig_ref[...])
    field_high, field_low = split2(structure[...])
    ewald = (
        jnp.dot(waves_high, field_high, preferred_element_type=F32)
        + jnp.dot(waves_low, field_high, preferred_element_type=F32)
        + jnp.dot(waves_high, field_low, preferred_element_type=F32)
    ) * SCALE
    mid_s = sp_ref[base, 0:BS, :] + ds_ref[...] + ewald
    mid_v = [v_ref[base, d] + dv_ref[d] for d in range(3)]
    mixing = jnp.concatenate([right3(ml_ref[...]), right3(mr_ref[...])], axis=1)
    mixed = dot3(jnp.concatenate(mid_v, axis=0), mixing)
    lefts = [mixed[d * BS : (d + 1) * BS, :BS] for d in range(3)]
    rights = [mixed[d * BS : (d + 1) * BS, BS:] for d in range(3)]
    norm = jnp.sqrt(rights[0] * rights[0] + rights[1] * rights[1] + rights[2] * rights[2] + 1.0)
    inner = lefts[0] * rights[0] + lefts[1] * rights[1] + lefts[2] * rights[2]
    hidden = dot3(jnp.concatenate([mid_s, norm], axis=1), right3(ui_ref[...]))
    hidden = hidden / (1.0 + jnp.exp(-hidden))
    gates = dot3(hidden, right3(uo_ref[...]))
    out_s_ref[0:BS, :] = mid_s + gates[:, BS : 2 * BS] * inner + gates[:, 2 * BS :]
    if layer < LAYERS - 1:
        out_s_ref[BS : BS + 8, :] = sp_ref[base, BS : BS + 8, :]
    for d in range(3):
        out_v_ref[d] = mid_v[d] + gates[:, :BS] * lefts[d]


def pair_layer(layer, n_region, pair_blocks, masks, sp_all, v_all, st, own_trig, weights):
    vmem = pl.BlockSpec(memory_space=pltpu.VMEM)
    hbm = pl.BlockSpec(memory_space=pltpu.HBM)
    rows = SROWS if layer < LAYERS - 1 else BS
    pairs = pair_blocks.shape[1] // n_region
    return pl.pallas_call(
        functools.partial(pair_kernel, layer, n_region),
        out_shape=(
            jax.ShapeDtypeStruct((rows, BS), F32),
            jax.ShapeDtypeStruct((3, BS, BS), F32),
        ),
        in_specs=[hbm] * 2 + [vmem] * 4 + [hbm] * len(weights),
        out_specs=(vmem, vmem),
        scratch_shapes=[
            pltpu.SMEM(pair_blocks.shape, jnp.int32),
            pltpu.VMEM((pairs, masks.shape[1]), jnp.int32),
        ]
        + [pltpu.VMEM(w.shape[1:], F32) for w in weights]
        + [
            pltpu.SemaphoreType.DMA((len(weights) + 2,)),
            pltpu.VMEM((BS, BS), F32),
            pltpu.VMEM((3, BS, BS), F32),
            pltpu.VMEM((2 * KW, BS), F32),
            pltpu.VMEM((256, ROWS15 * BS), BF16),
            pltpu.VMEM((3 * BS, BS), BF16),
            pltpu.VMEM((3 * BS, 3 * BS), BF16),
            pltpu.VMEM((NRBF, 4 * BS), F32),
            pltpu.VMEM((NRBF, 4 * BS), F32),
            pltpu.VMEM((2, 16 * ROWS15, BS), F32),
            pltpu.VMEM((4 * BS, 4 * BS), BF16),
            pltpu.VMEM((4 * BS, 4 * BS), BF16),
            pltpu.VMEM((NRBF * BS, 4 * BS), BF16),
            pltpu.VMEM((NRBF * BS, 4 * BS), BF16),
            pltpu.VMEM((BS, 4 * BS), F32),
            pltpu.VMEM((BS, 4 * BS), F32),
            pltpu.SMEM((2, pairs + 8), jnp.int32),
        ],
        compiler_params=pltpu.CompilerParams(vmem_limit_bytes=PAIR_VMEM),
        name="pair_layer",
    )(
        pair_blocks,
        masks,
        sp_all,
        v_all,
        st,
        own_trig,
        *weights,
    )


def body(
    scalars,
    vectors,
    positions,
    pair_blocks,
    pair_mask,
    wavevectors,
    message_in,
    message_out,
    filter_weight,
    ewald_weight,
    ewald_filter,
    mixing_left,
    mixing_right,
    update_in,
    update_out,
):
    n_region = lax.axis_size("region")
    weights = (
        message_in,
        message_out,
        filter_weight,
        ewald_filter,
        mixing_left,
        mixing_right,
        update_in,
        update_out,
    )
    weights = [far(w) for w in weights]
    pair_blocks, masks = far(pair_blocks), far(pair_mask)
    sp_all, v_all, st, trig, own_trig = exchange(
        True, 0, far(scalars), far(positions), far(vectors), far(wavevectors), far(ewald_weight)
    )
    sp, v_now = pair_layer(
        0, n_region, pair_blocks, masks, sp_all, v_all, st, own_trig, weights
    )
    sp_all, v_all, st = exchange(False, 1, sp, v_now, trig, far(ewald_weight))
    return pair_layer(
        1, n_region, pair_blocks, masks, sp_all, v_all, st, own_trig, weights
    )


def solution(mesh):
    placed = (
        P(("region", "sub"), None),
        P(None, ("region", "sub"), None),
        P(None, ("region", "sub")),
    ) + (P(),) * 12
    return jax.shard_map(
        body,
        mesh=mesh,
        in_specs=placed,
        out_specs=(P(("region", "sub"), None), P(None, ("region", "sub"), None)),
        check_vma=False,
    )
```

```python
import functools
import math

import jax
import jax.numpy as jnp
from jax import lax
from jax.experimental import pallas as pl
from jax.experimental.pallas import tpu as pltpu
from jax.sharding import PartitionSpec as P

NRBF = 20
BS = 128
KW = 512
LAYERS = 2
CUTOFF = 8.0
SPACING = CUTOFF / (NRBF - 1)
CENTRE = 4.0
ROWS15 = 15
RATE = math.sqrt(0.5 * math.log2(math.e))
KCHUNK = 5
READY = 4
SCALE = 1.0 / math.sqrt(16384 * KW)

BF16 = jnp.bfloat16
F32 = jnp.float32


def far(x):
    return pltpu.with_memory_space_constraint(x, pltpu.HBM)


def split2(x):
    high = x.astype(BF16)
    low = (x - high.astype(F32)).astype(BF16)
    return high, low


def left3(x):
    high, low = split2(x)
    return jnp.concatenate([high, low, high], axis=1)


def right3(x):
    high, low = split2(x)
    return jnp.concatenate([high, high, low], axis=0)


def dot3(x, weights):
    return jnp.dot(left3(x), weights, preferred_element_type=F32)


EXCHANGE_VMEM = 8 << 20
PAIR_VMEM = 22 << 20
MESH = pl.DeviceIdType.MESH
HALF = BS // 2
SROWS = BS + 8


def waves_of(phase):
    count = jnp.floor(phase * (2.0 / math.pi) + 0.5)
    rest = phase - count * 1.5703125
    rest = rest - count * 4.837512969970703125e-4
    rest = rest - count * 7.549789948768648e-8
    square = rest * rest
    sine = rest + rest * square * (
        -1.6666654611e-1 + square * (8.3321608736e-3 - square * 1.9515295891e-4)
    )
    cosine = (
        1.0
        - 0.5 * square
        + square
        * square
        * (4.166664568298827e-2 + square * (-1.388731625493765e-3 + square * 2.443315711809948e-5))
    )

    def pick(ahead):
        quarter = count + ahead
        half = jnp.floor(quarter * 0.5)
        odd = quarter - 2.0 * half
        sign = 1.0 - 2.0 * (half - 2.0 * jnp.floor(half * 0.5))
        return sign * (sine + odd * (cosine - sine))

    return pick(1.0), pick(0.0)


def mask_plan():
    flat = lax.broadcasted_iota(jnp.int32, (1, ROWS15 * BS), 1)
    word = (flat * 2185) >> 16
    bit = flat - word * 30
    return (bit >> 3) * 64 + word, bit & 7


def fill_onehot(onehot, column):
    onehot[...] = jnp.where(
        lax.broadcasted_iota(jnp.int32, (256, ROWS15 * BS), 0) == column, 1.0, 0.0
    ).astype(BF16)


def unpack_mask(line, onehot, shift, pad_ref):
    low_lane = lax.broadcasted_iota(jnp.int32, (8, BS), 1) < 64
    short = line.shape[1] - 4 * BS
    last = jnp.concatenate([line[:, 4 * BS :], jnp.zeros((1, BS - short), jnp.int32)], axis=1)
    words = jnp.concatenate(
        [line[:, n * BS : (n + 1) * BS] for n in range(4)] + [last] * 4, axis=0
    )
    bytes4 = [((words >> (8 * q)) & 255).astype(F32) for q in range(4)]
    turned = [pltpu.roll(x, 64, 1) for x in bytes4]
    even = [jnp.where(low_lane, bytes4[q], turned[q + 1]) for q in (0, 2)]
    odd = [jnp.where(low_lane, turned[q], bytes4[q + 1]) for q in (0, 2)]
    packed = jnp.concatenate(
        [jnp.concatenate(even, axis=1), jnp.concatenate(odd, axis=1)], axis=0
    ).astype(BF16)
    found = jnp.dot(packed, onehot[...], preferred_element_type=F32)
    bits = ((found.astype(jnp.int32) >> shift) & 1).astype(F32)
    for r in range(ROWS15):
        for n in range(2):
            pad_ref[pl.ds(n * ROWS15 + r, 8, stride=2 * ROWS15), :] = bits[
                n * 8 : n * 8 + 8, r * BS : (r + 1) * BS
            ]
    return pad_ref[0:BS, :]


def pair_shape(plain, straight, alive, pos_src, col_rcv):
    mask = (straight * alive) * plain + ((1.0 - straight) * alive) * plain.T
    square = None
    for d in range(3):
        off = pos_src[d : d + 1, :] - col_rcv[:, d : d + 1]
        square = off * off if square is None else square + off * off
    distance = jnp.sqrt(square + 1.0)
    return jnp.where(mask > 0.5, distance * (RATE / SPACING), 1.0e4), 1.0 / distance


def radial_into(left_a, left_b, side, ks, scaled, inverse):
    lo = side * BS
    for k in ks:
        away = scaled - RATE * k
        decay = jnp.exp2(-(away * away))
        for left, value in ((left_a, decay), (left_b, decay * inverse)):
            high, low = split2(value)
            left[k * BS : (k + 1) * BS, lo : lo + BS] = high
            left[k * BS : (k + 1) * BS, 2 * BS + lo : 2 * BS + lo + BS] = low


def exchange_kernel(first_layer, layer, *refs):
    if first_layer:
        (s_hbm, pos_hbm, v_hbm, wide_hbm, ew_hbm) = refs[:5]
        (sp_all, v_all, s_all, trig, own_trig) = refs[5:10]
        rest = refs[10:]
        (wide_ref, wave_ref) = rest[-2:]
        rest = rest[:-2]
    else:
        (sp_ref, v_ref, trig, ew_hbm) = refs[:4]
        (sp_all, v_all, s_all) = refs[4:7]
        rest = refs[7:]
    (cross, ew_ref, send_sem, recv_sem, own_sem, x_send, x_recv, p_send, p_recv) = rest
    region = lax.axis_index("region")
    sub = lax.axis_index("sub")
    keep = [pltpu.make_async_copy(ew_hbm.at[layer], ew_ref, own_sem.at[0])]
    if first_layer:
        fetch = [
            pltpu.make_async_copy(s_hbm, sp_all.at[sub, pl.ds(0, BS), :], own_sem.at[1]),
            pltpu.make_async_copy(pos_hbm, sp_all.at[sub, pl.ds(BS, 3), :], own_sem.at[2]),
            pltpu.make_async_copy(v_hbm, v_all.at[sub], own_sem.at[3]),
            pltpu.make_async_copy(wide_hbm, wide_ref, own_sem.at[4]),
        ]
    else:
        fetch = []
        keep.append(pltpu.make_async_copy(sp_ref, sp_all.at[sub], own_sem.at[1]))
        keep.append(pltpu.make_async_copy(v_ref, v_all.at[sub], own_sem.at[2]))
    for copy in keep + fetch:
        copy.start()
    core = lax.rem(sub, 2)
    z = lax.rem(sub // 2, 4)
    y = sub // 8
    fwd = 1 + 2 * core
    bwd = 3 - 2 * core

    def device(dy, dz, other=False):
        use = 1 - core if other else core
        return (lax.rem(y + dy, 4) * 4 + lax.rem(z + dz, 4)) * 2 + use

    def place(half, one, two):
        return device(two, one) if half == 0 else device(one, two)

    partner = device(0, 0, True)
    barrier = pltpu.get_barrier_semaphore()
    peers = [(region, partner)]
    for step in range(1, 4):
        peers.append((region, device(step, 0)))
        peers.append((region, device(0, step)))
        peers.append((lax.rem(region + step, 4), sub))
    for peer in peers:
        pl.semaphore_signal(barrier, inc=1, device_id=peer, device_id_type=MESH)
    pl.semaphore_wait(barrier, len(peers))

    def piece(kind, half, dev):
        if kind == 0:
            if half == 0:
                return sp_all.at[dev, pl.ds(0, HALF), :]
            return sp_all.at[dev, pl.ds(HALF, SROWS - HALF), :]
        return v_all.at[dev, :, pl.ds(half * HALF, HALF), :]

    def own_piece(kind, half):
        if kind == 0:
            if half == 0:
                return sp_ref.at[pl.ds(0, HALF), :]
            return sp_ref.at[pl.ds(HALF, SROWS - HALF), :]
        return v_ref.at[:, pl.ds(half * HALF, HALF), :]

    sent = []

    def send(kind, half, dev, target, own=False):
        copy = pltpu.make_async_remote_copy(
            src_ref=own_piece(kind, half) if own and not first_layer else piece(kind, half, dev),
            dst_ref=piece(kind, half, dev),
            send_sem=send_sem.at[len(sent)],
            recv_sem=recv_sem.at[kind * 2 + half, dev],
            device_id=(region, target),
            device_id_type=MESH,
        )
        copy.start()
        sent.append(copy)

    def arrive(kind, half, dev):
        pltpu.make_async_remote_copy(
            src_ref=piece(kind, half, dev),
            dst_ref=piece(kind, half, dev),
            send_sem=send_sem.at[0],
            recv_sem=recv_sem.at[kind * 2 + half, dev],
            device_id=(region, partner),
            device_id_type=MESH,
        ).wait_recv()

    def own_sends(kind, stage):
        for half in range(2):
            for way in (fwd, bwd):
                target = place(half, way, 0) if stage == 0 else place(half, 0, way)
                send(kind, half, sub, target, own=True)

    def own_partner(kind):
        for half in range(2):
            send(kind, half, sub, partner, own=True)

    def second(kind, half, dev):
        send(kind, half, dev, place(half, 0, fwd))
        send(kind, half, dev, place(half, 0, bwd))
        send(kind, half, dev, partner)

    def near_first(kind, ways_now):
        for half in range(2):
            for way in ways_now:
                dev = place(half, way, 0)
                arrive(kind, half, dev)
                if kind == 0 and way is bwd:
                    send(kind, half, dev, place(half, fwd, 0))
                if kind == 1 and way is fwd:
                    send(kind, half, dev, place(half, bwd, 0))
                second(kind, half, dev)

    def far_first(kind):
        for half in range(2):
            dev = place(half, 2, 0)
            arrive(kind, half, dev)
            second(kind, half, dev)

    def near_second(kind, one):
        for half in range(2):
            dev = place(half, one, bwd)
            arrive(kind, half, dev)
            if kind == 0:
                send(kind, half, dev, place(half, 0, fwd))
            send(kind, half, dev, partner)
            dev = place(half, one, fwd)
            arrive(kind, half, dev)
            if kind == 1:
                send(kind, half, dev, place(half, 0, bwd))
            send(kind, half, dev, partner)

    def far_second(kind, one):
        for half in range(2):
            dev = place(half, one, 2)
            arrive(kind, half, dev)
            send(kind, half, dev, partner)

    def from_partner(kind):
        for half in range(2):
            for dy in range(4):
                for dz in range(4):
                    arrive(kind, half, device(dy, dz, True))

    slot = core * 16 + y * 4 + z
    for copy in fetch[:2]:
        copy.wait()
    own_sends(0, 0)
    own_sends(0, 1)
    own_partner(0)
    for copy in fetch[2:]:
        copy.wait()
    own_sends(1, 0)
    if first_layer:
        column = sp_all[sub, BS : BS + 8, :].T
        phase = (
            column[:, 0:1] * wide_ref[0:1, :]
            + column[:, 1:2] * wide_ref[1:2, :]
            + column[:, 2:3] * wide_ref[2:3, :]
        )
        cosines, sines = waves_of(phase)
        own_trig[:, 0:KW] = cosines
        own_trig[:, KW:] = sines
        wave_ref[...] = jnp.concatenate([wide_ref[...], jnp.zeros((5, KW), F32)], axis=0).T
    ways = (0, bwd, fwd, 2)
    near_first(0, (bwd, fwd))
    own_sends(1, 1)
    far_first(0)
    for one in ways[:3]:
        near_second(0, one)
    near_first(1, (fwd,))
    near_second(0, 2)
    near_first(1, (bwd,))
    own_partner(1)
    for one in ways:
        far_second(0, one)
    near_second(1, 0)
    for copy in keep:
        copy.wait()
    from_partner(0)
    far_first(1)
    if first_layer:
        wave = wave_ref[pl.ds(pl.multiple_of(slot * 16, 16), 16), :]

    def gather_structure(step, total):
        if first_layer:
            sides = []
            for n in range(2):
                pos = sp_all[2 * step + n, BS : BS + 8, :]
                phase = (
                    wave[:, 0:1] * pos[0:1, :]
                    + wave[:, 1:2] * pos[1:2, :]
                    + wave[:, 2:3] * pos[2:3, :]
                )
                sides.append(jnp.concatenate(waves_of(phase), axis=0))
            waves = jnp.concatenate(sides, axis=1)
            trig[step] = waves
        else:
            waves = trig[step]
        atoms = jnp.concatenate(
            [sp_all[2 * step, 0:BS, :], sp_all[2 * step + 1, 0:BS, :]], axis=0
        )
        wave_high, wave_low = split2(waves)
        atom_high, atom_low = split2(atoms)
        both = jnp.dot(
            jnp.concatenate([wave_high, wave_low], axis=0),
            atom_high,
            preferred_element_type=F32,
        )
        low = jnp.dot(wave_high, atom_low, preferred_element_type=F32)
        return total + (both[:32] + both[32:] + low)

    structure = lax.fori_loop(0, 16, gather_structure, jnp.zeros((32, BS), F32), unroll=4)
    cross[0] = dot3(structure, right3(ew_ref[...]))
    across = []
    for step in range(1, 4):
        copy = pltpu.make_async_remote_copy(
            src_ref=cross.at[0],
            dst_ref=cross.at[4 - step],
            send_sem=x_send.at[step - 1],
            recv_sem=x_recv.at[4 - step - 1],
            device_id=(lax.rem(region + step, 4), sub),
            device_id_type=MESH,
        )
        copy.start()
        across.append(copy)
    for one in ways[1:3]:
        near_second(1, one)
    for copy in across:
        copy.wait()
    s_all[slot] = cross[0] + cross[1] + cross[2] + cross[3]
    line = []
    for step in range(1, 4):
        copy = pltpu.make_async_remote_copy(
            src_ref=s_all.at[slot],
            dst_ref=s_all.at[slot],
            send_sem=p_send.at[step - 1],
            recv_sem=p_recv.at[step - 1],
            device_id=(region, device(0, step)),
            device_id_type=MESH,
        )
        copy.start()
        line.append(copy)
    near_second(1, 2)
    for copy in line:
        copy.wait()
    plane = []
    mine = s_all.at[pl.ds(core * 16 + y * 4, 4)]
    for step in range(1, 4):
        copy = pltpu.make_async_remote_copy(
            src_ref=mine,
            dst_ref=mine,
            send_sem=p_send.at[2 + step],
            recv_sem=p_recv.at[2 + step],
            device_id=(region, device(step, 0)),
            device_id_type=MESH,
        )
        copy.start()
        plane.append(copy)
    for one in ways:
        far_second(1, one)
    for copy in plane:
        copy.wait()
    side = s_all.at[pl.ds(core * 16, 16)]
    last = pltpu.make_async_remote_copy(
        src_ref=side,
        dst_ref=side,
        send_sem=p_send.at[6],
        recv_sem=p_recv.at[6],
        device_id=(region, partner),
        device_id_type=MESH,
    )
    last.start()
    from_partner(1)
    last.wait()
    for copy in sent:
        copy.wait_send()


SENDS = 124


def exchange(first_layer, layer, *args):
    vmem = pl.BlockSpec(memory_space=pltpu.VMEM)
    hbm = pl.BlockSpec(memory_space=pltpu.HBM)
    shapes = [(32, SROWS, BS), (32, 3, BS, BS), (32, 32, BS)]
    if first_layer:
        shapes += [(16, 32, 2 * BS), (BS, 2 * KW)]
    return pl.pallas_call(
        functools.partial(exchange_kernel, first_layer, layer),
        out_shape=tuple(jax.ShapeDtypeStruct(shape, F32) for shape in shapes),
        in_specs=[hbm] * 5 if first_layer else [vmem] * 3 + [hbm],
        out_specs=(vmem,) * len(shapes),
        scratch_shapes=[
            pltpu.VMEM((4, 32, BS), F32),
            pltpu.VMEM((BS, BS), F32),
            pltpu.SemaphoreType.DMA((SENDS,)),
            pltpu.SemaphoreType.DMA((4, 32)),
            pltpu.SemaphoreType.DMA((5,)),
            pltpu.SemaphoreType.DMA((3,)),
            pltpu.SemaphoreType.DMA((3,)),
            pltpu.SemaphoreType.DMA((7,)),
            pltpu.SemaphoreType.DMA((7,)),
        ]
        + ([pltpu.VMEM((3, KW), F32), pltpu.VMEM((KW, 8), F32)] if first_layer else []),
        compiler_params=pltpu.CompilerParams(
            collective_id=layer, has_side_effects=True, vmem_limit_bytes=EXCHANGE_VMEM
        ),
        name="exchange_first" if first_layer else "exchange_next",
    )(*args)


def pair_kernel(layer, n_region, *refs):
    refs = list(refs)
    if layer == 0:
        refs[6:6] = [refs.pop(16), refs.pop(16)]
    (
        pb_hbm,
        mask_hbm,
        sp_ref,
        v_ref,
        st_ref,
        trig_ref,
        ready_a,
        ready_b,
        w1_hbm,
        w2_hbm,
        filt_hbm,
        ef_hbm,
        ml_hbm,
        mr_hbm,
        ui_hbm,
        uo_hbm,
        out_s_ref,
        out_v_ref,
        pb_ref,
        mask_ref,
        w1_ref,
        w2_ref,
        filt_ref,
        ef_ref,
        ml_ref,
        mr_ref,
        ui_ref,
        uo_ref,
        sem,
        ds_ref,
        dv_ref,
        structure,
        onehot,
        w1c,
        w2c,
        filt_a,
        filt_b,
        mask_pad,
        src_a,
        src_b,
        left_a,
        left_b,
        acc_a,
        acc_b,
        todo,
    ) = refs
    pairs = pb_hbm.shape[1] // n_region
    region = lax.axis_index("region")
    base = lax.axis_index("sub")
    list_move = pltpu.make_async_copy(pb_hbm, pb_ref, sem.at[8])
    list_move.start()
    mask_move = pltpu.make_async_copy(mask_hbm.at[pl.ds(region * pairs, pairs)], mask_ref, sem.at[9])
    mask_move.start()
    moves = []
    for n, (far, near) in enumerate(
        (
            (w1_hbm, w1_ref),
            (w2_hbm, w2_ref),
            (filt_hbm, filt_ref),
            (ef_hbm, ef_ref),
            (ml_hbm, ml_ref),
            (mr_hbm, mr_ref),
            (ui_hbm, ui_ref),
            (uo_hbm, uo_ref),
        )
    ):
        move = pltpu.make_async_copy(far.at[layer], near, sem.at[n])
        move.start()
        moves.append(move)
    blocks = sp_ref.shape[0]
    rows = BS
    column, shift = mask_plan()
    ds_ref[...] = jnp.zeros_like(ds_ref)
    dv_ref[...] = jnp.zeros_like(dv_ref)
    list_move.wait()

    def listing(pair, count):
        first = pb_ref[0, region * pairs + pair] - region * blocks
        second = pb_ref[1, region * pairs + pair] - region * blocks

        @pl.when(first == base)
        def _():
            todo[0, count] = second
            todo[1, count] = pair

        @pl.when(second == base)
        def _():
            todo[0, count] = first
            todo[1, count] = pair

        return count + ((first == base) | (second == base)).astype(jnp.int32)

    count = lax.fori_loop(0, pairs, listing, 0)
    todo[0, count] = base
    todo[1, count] = 0
    mask_move.wait()
    for move in moves[:3]:
        move.wait()
    w1c[...] = right3(w1_ref[...])
    w2c[...] = right3(w2_ref[...])
    filt = filt_ref[...]
    filt_a[...] = jnp.concatenate([filt[:, :BS]] + [filt[:, BS : 2 * BS]] * 3, axis=1)
    filt_b[...] = jnp.concatenate([filt[:, 2 * BS :]] * 4, axis=1)
    pos_rcv = sp_ref[base, BS : BS + 8, :]
    col_rcv = pos_rcv.T

    def fill_sources(term, side):
        source = todo[0, term]
        hidden = dot3(sp_ref[source, 0:BS, :], w1c[...])
        hidden = hidden / (1.0 + jnp.exp(-hidden))
        phi = dot3(hidden, w2c[...])
        col_src = sp_ref[source, BS : BS + 8, :].T
        phi_v = phi[:, BS : 2 * BS]
        phi_r = phi[:, 2 * BS :]
        parts = [phi[:, :BS]]
        for d in range(3):
            parts.append(phi_v * v_ref[source, d])
        for d in range(3):
            parts.append(phi_r * (col_src[:, d : d + 1] - CENTRE))
        parts.append(phi_r)
        lo = side * BS
        for n, part in enumerate(parts):
            src = src_a if n < 4 else src_b
            high, low = split2(part)
            at = (n % 4) * BS
            src[lo : lo + BS, at : at + BS] = high
            src[2 * BS + lo : 2 * BS + lo + BS, at : at + BS] = low

    def multiply(chunk, lefts):
        for acc, left, src, filters in (
            (acc_a, lefts[0], src_a, filt_a),
            (acc_b, lefts[1], src_b, filt_b),
        ):
            high = src[0 : 2 * BS, :]
            weights = jnp.concatenate([high, high, src[2 * BS :, :]], axis=0)
            lo = chunk * KCHUNK
            block = left[lo * rows : (lo + KCHUNK) * rows, :]
            product = jnp.dot(
                jnp.concatenate([block, block[:, : 2 * BS]], axis=1),
                weights,
                preferred_element_type=F32,
            )
            total = None
            for k in range(KCHUNK):
                term = product[k * rows : (k + 1) * rows, :] * filters[lo + k : lo + k + 1, :]
                total = term if total is None else total + term
            if chunk == 0:
                acc[...] = total
            else:
                acc[...] += total

    def collect():
        ds_ref[...] += acc_a[:, :BS]
        tail = acc_b[:, 3 * BS :]
        for d in range(3):
            dv_ref[d] += (
                acc_a[:, (d + 1) * BS : (d + 2) * BS]
                + acc_b[:, d * BS : (d + 1) * BS]
                - (col_rcv[:, d : d + 1] - CENTRE) * tail
            )

    def visit_ready(step, carry):
        for side in range(2):
            fill_sources(2 * step + side, side)
        for chunk in range(NRBF // KCHUNK):
            multiply(chunk, (ready_a.at[step], ready_b.at[step]))
        collect()
        return carry

    def visit_rest(step, carry, store=False):
        left_now = (ready_a.at[step], ready_b.at[step]) if store else (left_a, left_b)
        shapes = []
        for side in range(2):
            term = 2 * step + side
            fill_sources(term, side)
            source = todo[0, term]
            plain = unpack_mask(
                mask_ref[pl.ds(todo[1, term], 1), :], onehot, shift, mask_pad.at[side]
            )
            shapes.append(
                pair_shape(
                    plain,
                    (source > base).astype(F32),
                    (term < count).astype(F32),
                    sp_ref[source, BS : BS + 8, :],
                    col_rcv,
                )
            )
        for chunk in range(NRBF // KCHUNK):
            ks = range(chunk * KCHUNK, (chunk + 1) * KCHUNK)
            for side in range(2):
                radial_into(*left_now, side, ks, *shapes[side])
            multiply(chunk, left_now)
        collect()
        return carry

    steps = (count + 1) // 2
    if layer == 0:
        fill_onehot(onehot, column)
        visit_early = functools.partial(visit_rest, store=True)
    else:
        visit_early = visit_ready
    lax.fori_loop(0, jnp.minimum(steps, READY), visit_early, 0)

    @pl.when(steps > READY)
    def _():
        fill_onehot(onehot, column)
        lax.fori_loop(READY, steps, visit_rest, 0)

    for move in moves[3:]:
        move.wait()
    for n in range(32):
        for side in range(2):
            lo = side * KW + n * 16
            structure[lo : lo + 16, :] = (
                st_ref[n, side * 16 : side * 16 + 16, :] * ef_ref[n * 16 : n * 16 + 16, :]
            )
    waves_high, waves_low = split2(trig_ref[...])
    field_high, field_low = split2(structure[...])
    ewald = (
        jnp.dot(waves_high, field_high, preferred_element_type=F32)
        + jnp.dot(waves_low, field_high, preferred_element_type=F32)
        + jnp.dot(waves_high, field_low, preferred_element_type=F32)
    ) * SCALE
    mid_s = sp_ref[base, 0:BS, :] + ds_ref[...] + ewald
    mid_v = [v_ref[base, d] + dv_ref[d] for d in range(3)]
    mixing = jnp.concatenate([right3(ml_ref[...]), right3(mr_ref[...])], axis=1)
    mixed = dot3(jnp.concatenate(mid_v, axis=0), mixing)
    lefts = [mixed[d * BS : (d + 1) * BS, :BS] for d in range(3)]
    rights = [mixed[d * BS : (d + 1) * BS, BS:] for d in range(3)]
    norm = jnp.sqrt(rights[0] * rights[0] + rights[1] * rights[1] + rights[2] * rights[2] + 1.0)
    inner = lefts[0] * rights[0] + lefts[1] * rights[1] + lefts[2] * rights[2]
    hidden = dot3(jnp.concatenate([mid_s, norm], axis=1), right3(ui_ref[...]))
    hidden = hidden / (1.0 + jnp.exp(-hidden))
    gates = dot3(hidden, right3(uo_ref[...]))
    out_s_ref[0:BS, :] = mid_s + gates[:, BS : 2 * BS] * inner + gates[:, 2 * BS :]
    if layer < LAYERS - 1:
        out_s_ref[BS : BS + 8, :] = sp_ref[base, BS : BS + 8, :]
    for d in range(3):
        out_v_ref[d] = mid_v[d] + gates[:, :BS] * lefts[d]


def pair_layer(layer, n_region, pair_blocks, masks, sp_all, v_all, st, kept, weights):
    vmem = pl.BlockSpec(memory_space=pltpu.VMEM)
    hbm = pl.BlockSpec(memory_space=pltpu.HBM)
    rows = SROWS if layer < LAYERS - 1 else BS
    pairs = pair_blocks.shape[1] // n_region
    cached = (jax.ShapeDtypeStruct((READY, NRBF * BS, 4 * BS), BF16),) * (2 if layer == 0 else 0)
    return pl.pallas_call(
        functools.partial(pair_kernel, layer, n_region),
        out_shape=(
            jax.ShapeDtypeStruct((rows, BS), F32),
            jax.ShapeDtypeStruct((3, BS, BS), F32),
        )
        + cached,
        in_specs=[hbm] * 2 + [vmem] * (3 + len(kept)) + [hbm] * len(weights),
        out_specs=(vmem, vmem) + (vmem,) * len(cached),
        scratch_shapes=[
            pltpu.SMEM(pair_blocks.shape, jnp.int32),
            pltpu.VMEM((pairs, masks.shape[1]), jnp.int32),
        ]
        + [pltpu.VMEM(w.shape[1:], F32) for w in weights]
        + [
            pltpu.SemaphoreType.DMA((len(weights) + 2,)),
            pltpu.VMEM((BS, BS), F32),
            pltpu.VMEM((3, BS, BS), F32),
            pltpu.VMEM((2 * KW, BS), F32),
            pltpu.VMEM((256, ROWS15 * BS), BF16),
            pltpu.VMEM((3 * BS, BS), BF16),
            pltpu.VMEM((3 * BS, 3 * BS), BF16),
            pltpu.VMEM((NRBF, 4 * BS), F32),
            pltpu.VMEM((NRBF, 4 * BS), F32),
            pltpu.VMEM((2, 16 * ROWS15, BS), F32),
            pltpu.VMEM((4 * BS, 4 * BS), BF16),
            pltpu.VMEM((4 * BS, 4 * BS), BF16),
            pltpu.VMEM((NRBF * BS, 4 * BS), BF16),
            pltpu.VMEM((NRBF * BS, 4 * BS), BF16),
            pltpu.VMEM((BS, 4 * BS), F32),
            pltpu.VMEM((BS, 4 * BS), F32),
            pltpu.SMEM((2, pairs + 8), jnp.int32),
        ],
        compiler_params=pltpu.CompilerParams(vmem_limit_bytes=PAIR_VMEM),
        name="pair_layer",
    )(
        pair_blocks,
        masks,
        sp_all,
        v_all,
        st,
        *kept,
        *weights,
    )


def body(
    scalars,
    vectors,
    positions,
    pair_blocks,
    pair_mask,
    wavevectors,
    message_in,
    message_out,
    filter_weight,
    ewald_weight,
    ewald_filter,
    mixing_left,
    mixing_right,
    update_in,
    update_out,
):
    n_region = lax.axis_size("region")
    weights = (
        message_in,
        message_out,
        filter_weight,
        ewald_filter,
        mixing_left,
        mixing_right,
        update_in,
        update_out,
    )
    weights = [far(w) for w in weights]
    pair_blocks, masks = far(pair_blocks), far(pair_mask)
    sp_all, v_all, st, trig, own_trig = exchange(
        True, 0, far(scalars), far(positions), far(vectors), far(wavevectors), far(ewald_weight)
    )
    sp, v_now, *ready = pair_layer(
        0, n_region, pair_blocks, masks, sp_all, v_all, st, (own_trig,), weights
    )
    sp_all, v_all, st = exchange(False, 1, sp, v_now, trig, far(ewald_weight))
    return pair_layer(
        1, n_region, pair_blocks, masks, sp_all, v_all, st, (own_trig, *ready), weights
    )


def solution(mesh):
    placed = (
        P(("region", "sub"), None),
        P(None, ("region", "sub"), None),
        P(None, ("region", "sub")),
    ) + (P(),) * 12
    return jax.shard_map(
        body,
        mesh=mesh,
        in_specs=placed,
        out_specs=(P(("region", "sub"), None), P(None, ("region", "sub"), None)),
        check_vma=False,
    )
```
